128 devices in a mesh: branch: 2 (over y_hi), term: 64 (over z, x, y_lo, core).
Axes of the slice: x: 4, y: 4 (y_hi: 2, y_lo: 2; y = y_hi * 2 + y_lo), z: 4, core: 2. Of those that a mesh axis runs over, the one named last changes fastest.
Arguments:
- lower_nodes: float32 [2, 64, 64, 128], P('branch', 'term'), may hold values from -0.09375 to 0.09375
- upper_nodes: float32 [2, 64, 128, 128], P('branch', 'term'), may hold values from -0.0625 to 0.0625
- root_coefficient_grid: float32 [128, 128], replicated, may hold values from -0.5 to 0.5
- mode_ops: float32 [2, 3, 64, 2048], P('branch'), may hold values from -0.75 to 0.75
- op_table: int32 [128, 2, 3], P('term', 'branch'), may hold values from 0 to 31
- leaf_active: int32 [128, 2, 3], P('term', 'branch'), may hold values from 0 to 1, as said below
- term_coef: float32 [128], P('term'), may hold values from -48 to 48
Outputs:
- lower_grads: float32 [2, 64, 64, 128], P('branch', 'term')
- upper_grads: float32 [2, 64, 128, 128], P('branch', 'term')
- root_image: float32 [128, 128], replicated
The draws below stay inside these ranges and needn't reach their ends.
Inputs may be any that keep to these rules, and one draw needn't show every extreme that they name: `leaf_active`: 1 where the term's factor on that mode is its operator from op_table, 0 where the factor is the identity. `op_table`: index into the operators of mode_ops for that subtree and mode.
All inputs are finite; a program needn't handle non-finite values.
Results may differ from the reference program's by a relative error of at most 0.0003.
Values sent between devices are 32-bit elements; how exact they have to be, the bound alone decides.
No kernel may reach another device: no remote copies, remote signals or barrier semaphores. Data moves between devices by JAX's collectives and lax.ppermute only.
A program may use at most 128 MiB of HBM per device.

```python
import jax
import jax.numpy as jnp
from jax import lax

P_SIZE = 64
R = 128
NOPS = 32
TERMS = 128


def draw_leaf_active(key, part):
    term_number = jnp.arange(TERMS, dtype=jnp.int32)
    threshold = 150 + 800 * term_number // TERMS
    dice_rolls = jax.random.randint(key, (TERMS, 2, 3), 0, 1000, dtype=jnp.int32)
    return (dice_rolls < threshold[:, None, None]).astype(jnp.int32)


def with_ends(array, stream_key, least, top_value):
    place = [jax.random.randint(jax.random.fold_in(stream_key, axis), (), 0, length) for axis, length in enumerate(array.shape)]
    widest = array.shape.index(max(array.shape))
    neighbour = place[:widest] + [(place[widest] + 1) % array.shape[widest]] + place[widest + 1:]
    return array.at[tuple(place)].set(least).at[tuple(neighbour)].set(top_value)


def steps_of(own_key, dims, cuts, smallest, largest):
    gain, own = 1.0, jax.random.fold_in(own_key, 6)
    for dim, parts in cuts:
        draws = jnp.exp(jax.random.uniform(jax.random.fold_in(own, dim), (parts,), jnp.float32, smallest / len(cuts), largest / len(cuts)))
        gain = gain * jnp.repeat(draws, dims[dim] // parts).reshape([-1 if axis == dim else 1 for axis in range(len(dims))])
    return gain


def bell_draw(own_key, extent, width, most, shards=(), kind=jnp.bfloat16):
    factor_of = steps_of(own_key, extent, shards, -0.22, 0.18) if shards else 1.0
    drawn = jax.random.normal(own_key, extent, jnp.float32) * width * factor_of
    return jnp.minimum(jnp.maximum(drawn, -most), most).astype(kind)


def setup_inputs(seed: int = 0) -> dict:
    key_of = jax.random.split(jax.random.key(seed), 8)
    lower_nodes = bell_draw(key_of[0], (2, P_SIZE, P_SIZE, R), (P_SIZE * P_SIZE) ** -0.5, 0.09375, ((0, 2), (1, 64)), jnp.float32)
    upper_nodes = bell_draw(key_of[1], (2, P_SIZE, R, R), (P_SIZE * R) ** -0.5, 0.0625, ((0, 2), (1, 64)), jnp.float32)
    root_coefficient_grid = bell_draw(key_of[2], (R, R), R ** -0.5, 0.5, (), jnp.float32)
    mode_ops = bell_draw(key_of[3], (2, 3, P_SIZE, NOPS * P_SIZE), P_SIZE ** -0.5, 0.75, ((0, 2),), jnp.float32)
    op_table = with_ends(jax.random.randint(key_of[4], (TERMS, 2, 3), 0, NOPS), jax.random.fold_in(key_of[4], 1), 0, NOPS - 1).astype(jnp.int32)
    leaf_active = draw_leaf_active(jax.random.fold_in(key_of[7], 71), 0)
    term_coef = bell_draw(key_of[6], (TERMS,), 8.0, 48.0, ((0, 64),), jnp.float32)
    return dict(lower_nodes=lower_nodes, upper_nodes=upper_nodes, root_coefficient_grid=root_coefficient_grid, mode_ops=mode_ops, op_table=op_table, leaf_active=leaf_active, term_coef=term_coef)


TOP_PRECISION = lax.Precision.HIGHEST


def select_mode(library, op_index, active, mode_number):
    basis_size = library.shape[1]
    chosen = lax.dynamic_slice_in_dim(library[mode_number], (op_index[mode_number] * basis_size).astype(jnp.int32), basis_size, 1)
    identity = jnp.eye(basis_size, dtype=chosen.dtype)
    return jnp.where(active[mode_number] == 1, chosen, identity)


def lower_image(lower_node, first_mode, second_mode):
    full_shape = lower_node.shape
    partial_image = jnp.dot(first_mode, lower_node.reshape(full_shape[0], -1), precision=TOP_PRECISION).reshape(full_shape)
    return jnp.einsum('jl,ilc->ijc', second_mode, partial_image, precision=TOP_PRECISION)


def upper_image(upper_node, third_mode):
    return jnp.dot(third_mode, upper_node.reshape(upper_node.shape[0], -1), precision=TOP_PRECISION).reshape(upper_node.shape)


def climb(lower_node, upper_node, library, op_index, active):
    first_mode = select_mode(library, op_index, active, 0)
    second_mode = select_mode(library, op_index, active, 1)
    third_mode = select_mode(library, op_index, active, 2)
    image = lower_image(lower_node, first_mode, second_mode)
    level_two = jnp.einsum('ijc,ijd->cd', lower_node, image, precision=TOP_PRECISION)
    moved = upper_image(upper_node, third_mode)
    lifted = jnp.einsum('cd,kda->kca', level_two, moved, precision=TOP_PRECISION)
    level_one = jnp.einsum('kca,kcb->ab', upper_node, lifted, precision=TOP_PRECISION)
    return level_two, level_one


def descend(lower_node, upper_node, library, op_table, leaf_active, level_two, scaled_field):
    def descend_step(carried, term_data):
        upper_sum, lower_sum = carried
        op_index, active, level_op, field_term = term_data
        first_mode = select_mode(library, op_index, active, 0)
        second_mode = select_mode(library, op_index, active, 1)
        third_mode = select_mode(library, op_index, active, 2)
        moved = upper_image(upper_node, third_mode)
        weighted = jnp.dot(moved.reshape(-1, moved.shape[2]), field_term.T, precision=TOP_PRECISION).reshape(moved.shape)
        lower_field = jnp.einsum('kca,kda->cd', upper_node, weighted, precision=TOP_PRECISION)
        upper_term = jnp.einsum('cd,kda->kca', level_op, weighted, precision=TOP_PRECISION)
        image = lower_image(lower_node, first_mode, second_mode)
        lower_term = jnp.dot(image.reshape(-1, image.shape[2]), lower_field.T, precision=TOP_PRECISION).reshape(image.shape)
        return (upper_sum + upper_term, lower_sum + lower_term), None

    start_state = (jnp.zeros(upper_node.shape, upper_node.dtype), jnp.zeros(lower_node.shape, lower_node.dtype))
    (upper_sum, lower_sum), _ = lax.scan(descend_step, start_state, (op_table, leaf_active, level_two, scaled_field))
    return lower_sum, upper_sum


def reference(lower_nodes, upper_nodes, root_coefficient_grid, mode_ops, op_table, leaf_active, term_coef):
    def climb_step(carried, term_data):
        op_index, active = term_data
        first_pair = climb(lower_nodes[0], upper_nodes[0], mode_ops[0], op_index[0], active[0])
        second_pair = climb(lower_nodes[1], upper_nodes[1], mode_ops[1], op_index[1], active[1])
        return carried, (first_pair, second_pair)

    _, ((two_first, single_first_term), (two_second, single_second_term)) = lax.scan(
        climb_step, jnp.zeros((), jnp.int32), (op_table, leaf_active))
    middle_factor = jnp.einsum('qru,un->qrn', single_first_term, root_coefficient_grid, precision=TOP_PRECISION)
    term_products = jnp.einsum('jzv,jpv->jzp', middle_factor, single_second_term, precision=TOP_PRECISION)
    root_image = jnp.einsum('t,tad->ad', term_coef, term_products, precision=TOP_PRECISION)
    coefficient_column = term_coef[:, None, None]
    left_first_factor = jnp.einsum('gs,ysd->ygd', root_coefficient_grid, single_second_term, precision=TOP_PRECISION)
    first_subtree_field = coefficient_column * jnp.einsum('wqh,nh->wqn', left_first_factor, root_coefficient_grid, precision=TOP_PRECISION)
    flipped_matrix = root_coefficient_grid.T
    left_second_factor = jnp.einsum('gs,ysd->ygd', flipped_matrix, single_first_term, precision=TOP_PRECISION)
    second_subtree_field = coefficient_column * jnp.einsum('wqh,nh->wqn', left_second_factor, flipped_matrix, precision=TOP_PRECISION)
    lower_first, upper_first = descend(lower_nodes[0], upper_nodes[0], mode_ops[0], op_table[:, 0],
                                       leaf_active[:, 0], two_first, first_subtree_field)
    lower_second, upper_second = descend(lower_nodes[1], upper_nodes[1], mode_ops[1], op_table[:, 1],
                                         leaf_active[:, 1], two_second, second_subtree_field)
    return jnp.stack([lower_first, lower_second]), jnp.stack([upper_first, upper_second]), root_image
```

```python
import numpy as np
import jax
import jax.numpy as jnp
from jax import lax
from jax.sharding import PartitionSpec as P


PREC = lax.Precision.HIGH
EXACT = lax.Precision.HIGHEST


def dec(i):
    return i // 16, (i // 4) % 4, (i // 2) % 2, i % 2


def enc(z, x, y, c):
    return ((z % 4 * 4 + x % 4) * 2 + y) * 2 + c


def moved(i, second, first, dy, dc):
    z, x, y, c = dec(i)
    c = c ^ dc
    y = y ^ dy
    if c == 0:
        return enc(z + second, x + first, y, c)
    return enc(z + first, x + second, y, c)


def pairs_to(second, first, dy, dc):
    return [(i, moved(i, second, first, dy, dc)) for i in range(64)]


def send(value, second=0, first=0, dy=0, dc=0):
    return lax.ppermute(value, "term", pairs_to(second, first, dy, dc))


ORDER = np.array(
    [
        [moved(i, b, a, y, c) for c in range(2) for b in range(4) for a in range(4) for y in range(2)]
        for i in range(64)
    ],
    np.int32,
)


def gather_nodes(own):
    pair = jnp.stack([own, send(own, dy=1)])
    ring = jnp.stack([pair] + [send(pair, first=-a) for a in (1, 2, 3)])
    plane = [ring] + [send(ring, second=-b) for b in (1, 2, 3)]
    other = [send(block, dc=1) for block in plane]
    return jnp.stack(plane + other).reshape(64, 192, 128)


def reduce_nodes(blocks, root):
    root = root + send(root, dc=1)
    kept = [blocks[0, b] + send(blocks[1, b], dc=1) for b in range(4)]
    got = [
        send(jnp.concatenate([kept[b].reshape(-1, 128), root]), second=b) for b in (1, 2, 3)
    ]
    kept = kept[0] + sum(g[: 8 * 192].reshape(4, 2, 192, 128) for g in got)
    root = root + sum(g[8 * 192 :] for g in got)
    got = [
        send(jnp.concatenate([kept[a].reshape(-1, 128), root]), first=a) for a in (1, 2, 3)
    ]
    kept = kept[0] + sum(g[: 2 * 192].reshape(2, 192, 128) for g in got)
    root = root + sum(g[2 * 192 :] for g in got)
    got = send(jnp.concatenate([kept[1], root]), dy=1)
    return kept[0] + got[:192], root + got[192:]


def select_mode(library, op_index, active, mode_number):
    chosen = lax.dynamic_slice_in_dim(library[mode_number], op_index[mode_number] * 64, 64, 1)
    return jnp.where(active[mode_number] == 1, chosen, jnp.eye(64, dtype=chosen.dtype))


def local(
    lower_nodes, upper_nodes, root_coefficient_grid, mode_ops, op_table, leaf_active, term_coef
):
    own = jnp.concatenate([lower_nodes[0, 0], upper_nodes[0, 0]])
    nodes = gather_nodes(own)
    lower_node, upper_node = nodes[:, :64], nodes[:, 64:]
    order = jnp.asarray(ORDER)[lax.axis_index("term")]
    onehot = (order[:, None] == jnp.arange(64)[None, :]).astype(jnp.float32)

    def reorder(matrix):
        return jnp.einsum("ri,ij,sj->rs", onehot, matrix, onehot, precision=EXACT)

    first_mode, second_mode, third_mode = [], [], []
    for t in range(2):
        index, active = op_table[t, 0], leaf_active[t, 0]
        first_mode.append(reorder(select_mode(mode_ops[0], index, active, 0)))
        second_mode.append(select_mode(mode_ops[0], index, active, 1))
        third_mode.append(reorder(select_mode(mode_ops[0], index, active, 2)))
    first_mode, second_mode, third_mode = map(jnp.stack, (first_mode, second_mode, third_mode))

    half = jnp.einsum("til,ljc->tijc", first_mode, lower_node, precision=PREC)
    images = jnp.einsum("tjl,tilc->tijc", second_mode, half, precision=PREC)
    level_two = jnp.einsum("ijc,tijd->tcd", lower_node, images, precision=PREC)
    moveds = jnp.einsum("tkl,lca->tkca", third_mode, upper_node, precision=PREC)
    lifted = jnp.einsum("tcd,tkda->tkca", level_two, moveds, precision=PREC)
    level_one = jnp.einsum("kca,tkcb->tab", upper_node, lifted, precision=PREC)

    opposite = lax.ppermute(level_one, "branch", [(0, 1), (1, 0)])
    is_first = lax.axis_index("branch") == 0
    first_side = jnp.where(is_first, level_one, opposite)
    second_side = jnp.where(is_first, opposite, level_one)
    middle = jnp.einsum("qru,un->qrn", first_side, root_coefficient_grid, precision=PREC)
    products = jnp.einsum("jzv,jpv->jzp", middle, second_side, precision=PREC)
    root_part = jnp.sum(term_coef[:, None, None] * products, axis=0)
    aligned = jnp.where(is_first, root_coefficient_grid, root_coefficient_grid.T)
    left = jnp.einsum("gs,ysd->ygd", aligned, opposite, precision=PREC)
    field = term_coef[:, None, None] * jnp.einsum("wqh,nh->wqn", left, aligned, precision=PREC)

    weighted = jnp.einsum("tkca,tea->tkce", moveds, field, precision=PREC)
    lower_fields = jnp.einsum("kca,tkda->tcd", upper_node, weighted, precision=PREC)
    upper_sum = jnp.einsum("tkca,tea->kce", lifted, field, precision=PREC)
    lower_sum = jnp.einsum("tijd,tcd->ijc", images, lower_fields, precision=PREC)
    blocks = jnp.concatenate([lower_sum, upper_sum], axis=1).reshape(2, 4, 4, 2, 192, 128)
    grads, root_image = reduce_nodes(blocks, root_part)
    return grads[None, None, :64], grads[None, None, 64:], root_image


def solution(mesh):
    in_specs = (
        P("branch", "term", None, None),
        P("branch", "term", None, None),
        P(),
        P("branch", None, None, None),
        P("term", "branch", None),
        P("term", "branch", None),
        P("term"),
    )
    out_specs = (P("branch", "term", None, None), P("branch", "term", None, None), P())
    return jax.shard_map(local, mesh=mesh, in_specs=in_specs, out_specs=out_specs, check_vma=False)
```

```python
import numpy as np
import jax
import jax.numpy as jnp
from jax import lax
from jax.experimental import pallas as pl
from jax.experimental.pallas import tpu as pltpu
from jax.sharding import PartitionSpec as P


EXACT = lax.Precision.HIGHEST

F32, BF16 = jnp.float32, jnp.bfloat16
VM = 56 * 1024 * 1024
SL, SU = 72, 136


def split(x):
    hi = x.astype(BF16)
    return hi, (x - hi.astype(F32)).astype(BF16)


def dot(a, b):
    return lax.dot_general(a, b, (((1,), (0,)), ((), ())), preferred_element_type=F32)


def dot_nt(a, b):
    return lax.dot_general(a, b, (((1,), (1,)), ((), ())), preferred_element_type=F32)


def dot_tn(a, b):
    return lax.dot_general(a, b, (((0,), (0,)), ((), ())), preferred_element_type=F32)


def left3(x):
    hi, lo = split(x)
    return jnp.concatenate([hi, lo, hi], axis=1)


def right3(x):
    hi, lo = split(x)
    return jnp.concatenate([hi, hi, lo], axis=0)


def mm3(a, b):
    return dot(left3(a), right3(b))


def load_pairs(ref, base, rows, step):
    return jnp.concatenate([ref[pl.ds(base, rows)], ref[pl.ds(base + step, rows)]], axis=1)


def climb_kernel(m0, m1, m2, *refs):
    pieces = refs[:8]
    h1_out, h2_out, z_out, x_out = refs[8:12]
    low, upp, half, x_ref, z_ref, sems = refs[12:]
    low3 = low.reshape(65, SL, 128)
    upp3 = upp.reshape(65, SU, 128)
    z3 = z_ref.reshape(129, SU, 128)
    lows = [
        pltpu.make_async_copy(
            pieces[p].at[:, pl.ds(0, 64)], low3.at[pl.ds(8 * p, 8), pl.ds(0, 64)], sems.at[p]
        )
        for p in range(8)
    ]
    upps = [
        pltpu.make_async_copy(
            pieces[p].at[:, pl.ds(64, 128)], upp3.at[pl.ds(8 * p, 8), pl.ds(0, 128)], sems.at[8 + p]
        )
        for p in range(8)
    ]
    for c in lows + upps:
        c.start()
    a0 = left3(m0[...])
    a1 = [left3(m1[pl.ds(0, 64)]), left3(m1[pl.ds(64, 64)])]
    a2 = left3(m2[...])
    for c in lows:
        c.wait()

    def first_mode(s, carry):
        j = 2 * s
        both = jnp.concatenate(
            [low[pl.ds(j, 64, stride=SL)], low[pl.ds(j + 1, 64, stride=SL)]], axis=1
        )
        out = dot(a0, right3(both))
        half[pl.ds(j, 128, stride=SL), :] = out[:, :128]
        half[pl.ds(j + 1, 128, stride=SL), :] = out[:, 128:]
        return carry

    lax.fori_loop(0, 32, first_mode, 0, unroll=4)

    def second_mode(s, acc):
        i = 2 * s
        left = jnp.concatenate([low[pl.ds(i * SL, 64)], low[pl.ds(i * SL + SL, 64)]], axis=0)
        lhi, llo = split(left)
        xs = []
        for t in range(2):
            out = dot(a1[t], right3(load_pairs(half, (t * 64 + i) * SL, 64, SL)))
            x = jnp.concatenate([out[:, :128], out[:, 128:]], axis=0)
            x_ref[pl.ds(t * 4096 + i * 64, 128), :] = x
            xs.append(x)
        xhi, xlo = split(jnp.concatenate(xs, axis=1))
        return acc + dot_tn(
            jnp.concatenate([lhi, llo, lhi], axis=0), jnp.concatenate([xhi, xhi, xlo], axis=0)
        )

    h2 = lax.fori_loop(0, 32, second_mode, jnp.zeros((128, 256), F32), unroll=4)
    x_copy = pltpu.make_async_copy(x_ref, x_out, sems.at[16])
    x_copy.start()
    for c in upps:
        c.wait()

    def third_mode(s, carry):
        c = 2 * s
        both = jnp.concatenate(
            [upp[pl.ds(c, 64, stride=SU)], upp[pl.ds(c + 1, 64, stride=SU)]], axis=1
        )
        out = dot(a2, right3(both))
        z_ref[pl.ds(c, 128, stride=SU), :] = out[:, :128]
        z_ref[pl.ds(c + 1, 128, stride=SU), :] = out[:, 128:]
        return carry

    lax.fori_loop(0, 64, third_mode, 0, unroll=4)
    z_copies = [
        pltpu.make_async_copy(
            z3.at[pl.ds(16 * p, 16), pl.ds(0, 128)], z_out.at[pl.ds(16 * p, 16)], sems.at[17]
        )
        for p in range(8)
    ]
    for c in z_copies:
        c.start()
    h2_out[...] = h2
    b2 = [left3(h2[:, :128]), left3(h2[:, 128:])]

    def lift(s, acc):
        k = 2 * s
        ys = [dot(b2[t], right3(load_pairs(z_ref, (t * 64 + k) * SU, 128, SU))) for t in range(2)]
        for q in range(2):
            uhi, ulo = split(upp[pl.ds((k + q) * SU, 128)])
            y = jnp.concatenate([y[:, 128 * q : 128 * q + 128] for y in ys], axis=1)
            yhi, ylo = split(y)
            acc = acc + dot_tn(
                jnp.concatenate([uhi, ulo, uhi], axis=0), jnp.concatenate([yhi, yhi, ylo], axis=0)
            )
        return acc

    h1 = lax.fori_loop(0, 32, lift, jnp.zeros((128, 256), F32), unroll=2)
    h1_out[0] = h1[:, :128]
    h1_out[1] = h1[:, 128:]
    x_copy.wait()
    pltpu.make_async_copy(z3.at[pl.ds(0, 128), pl.ds(0, 128)], z_out, sems.at[17]).wait()


HBM_SPEC = pl.BlockSpec(memory_space=pl.ANY)
VMEM_SPEC = pl.BlockSpec(memory_space=pltpu.VMEM)
SMEM_SPEC = pl.BlockSpec(memory_space=pltpu.SMEM)


def climb(m0, m1, m2, pieces):
    return pl.pallas_call(
        climb_kernel,
        in_specs=[VMEM_SPEC] * 3 + [HBM_SPEC] * 8,
        out_specs=[VMEM_SPEC, VMEM_SPEC, HBM_SPEC, HBM_SPEC],
        out_shape=[
            jax.ShapeDtypeStruct((2, 128, 128), F32),
            jax.ShapeDtypeStruct((128, 256), F32),
            jax.ShapeDtypeStruct((128, 128, 128), F32),
            jax.ShapeDtypeStruct((8192, 128), F32),
        ],
        scratch_shapes=[
            pltpu.VMEM((65 * SL, 128), F32),
            pltpu.VMEM((65 * SU, 128), F32),
            pltpu.VMEM((129 * SL, 128), F32),
            pltpu.VMEM((8192, 128), F32),
            pltpu.VMEM((129 * SU, 128), F32),
            pltpu.SemaphoreType.DMA((18,)),
        ],
        compiler_params=pltpu.CompilerParams(vmem_limit_bytes=VM),
        name="climb",
    )(m0, m1, m2, *pieces)


def descend_kernel(info, coef, own, opposite, grid, h2, z_in, x_in, *refs):
    pieces = refs[:8]
    root_out = refs[8]
    outs = refs[9:17]
    upp, z_ref, x_ref, up_out, lo_out, sems = refs[17:]
    loads = []
    for p in range(8):
        group = [pltpu.make_async_copy(pieces[p].at[:, pl.ds(64, 128)], upp.at[pl.ds(8 * p, 8)], sems.at[p])]
        for t in range(2):
            rows = pl.ds(t * 64 + 8 * p, 8)
            group.append(pltpu.make_async_copy(z_in.at[rows], z_ref.at[rows], sems.at[p]))
        loads.append(group)
        for c in group:
            c.start()
    x_load = pltpu.make_async_copy(x_in, x_ref, sems.at[8])
    x_load.start()

    first = info[0] == 1
    g = grid[...]
    aligned = jnp.where(first, g, g.T)
    root = jnp.zeros((128, 128), F32)
    sides = []
    for t in range(2):
        mine, other = own[t], opposite[t]
        one = jnp.where(first, mine, other)
        two = jnp.where(first, other, mine)
        root = root + coef[t] * mm3(mm3(one, g), two.T)
        gt = coef[t] * mm3(aligned, mm3(aligned, other).T)
        hi, lo = split(gt)
        one = jnp.concatenate([hi, lo], axis=1)
        sides.append(jnp.concatenate([one, one], axis=0))
    root_out[...] = root

    hhi, hlo = split(h2[...])
    hs = jnp.concatenate([hhi, hlo], axis=0)

    def step(k, acc):
        ws = []
        for t in range(2):
            zz = jnp.concatenate([z_ref[t * 64 + k], z_ref[t * 64 + k + 1]], axis=0)
            hi, lo = split(zz)
            out = dot(jnp.concatenate([hi, lo], axis=1), sides[t])
            ws.append(out[:, :128] + out[:, 128:])
        w = jnp.concatenate(
            [jnp.concatenate([v[:128], v[128:]], axis=1) for v in ws], axis=0
        )
        whi, wlo = split(w)
        uhi, ulo = split(jnp.concatenate([upp[k], upp[k + 1]], axis=1))
        f = dot_nt(jnp.concatenate([uhi, ulo], axis=0), whi)
        acc = acc + f[:128] + f[128:] + dot_nt(uhi, wlo)
        up = dot(hs, whi)
        up = up[:128] + up[128:] + dot(hhi, wlo)
        up_out[k] = up[:, :128]
        up_out[k + 1] = up[:, 128:]
        return acc

    acc = jnp.zeros((128, 256), F32)
    stores = []
    for p in range(8):
        for c in loads[p]:
            c.wait()
        acc = lax.fori_loop(0, 4, lambda s, a: step(8 * p + 2 * s, a), acc, unroll=2)
        c = pltpu.make_async_copy(up_out.at[pl.ds(8 * p, 8)], outs[p].at[:, pl.ds(64, 128)], sems.at[9 + p])
        c.start()
        stores.append(c)
    hi, lo = split(acc.T)
    field = jnp.concatenate([hi, lo], axis=1)
    x_load.wait()
    for p in range(8):
        def low_step(s, carry):
            base = p * 512 + s * 256
            xhi, xlo = split(jnp.concatenate([x_ref[pl.ds(base, 256)], x_ref[pl.ds(4096 + base, 256)]], axis=1))
            a = dot(xhi, field)
            lo_out[pl.ds(base, 256)] = a[:, :128] + a[:, 128:] + dot(xlo, hi)
            return carry
        lax.fori_loop(0, 2, low_step, 0, unroll=2)
        c = pltpu.make_async_copy(
            lo_out.reshape(64, 64, 128).at[pl.ds(8 * p, 8)], outs[p].at[:, pl.ds(0, 64)], sems.at[17 + p]
        )
        c.start()
        stores.append(c)
    for c in stores:
        c.wait()


def descend(info, coef, own, opposite, grid, h2, z, x, pieces):
    return pl.pallas_call(
        descend_kernel,
        in_specs=[SMEM_SPEC] * 2 + [VMEM_SPEC] * 4 + [HBM_SPEC] * 10,
        out_specs=[VMEM_SPEC] + [HBM_SPEC] * 8,
        out_shape=[jax.ShapeDtypeStruct((128, 128), F32)]
        + [jax.ShapeDtypeStruct((8, 192, 128), F32)] * 8,
        scratch_shapes=[
            pltpu.VMEM((64, 128, 128), F32),
            pltpu.VMEM((128, 128, 128), F32),
            pltpu.VMEM((8192, 128), F32),
            pltpu.VMEM((64, 128, 128), F32),
            pltpu.VMEM((4096, 128), F32),
            pltpu.SemaphoreType.DMA((25,)),
        ],
        compiler_params=pltpu.CompilerParams(vmem_limit_bytes=VM),
        name="descend",
    )(info, coef, own, opposite, grid, h2, z, x, *pieces)


def dec(i):
    return i // 16, (i // 4) % 4, (i // 2) % 2, i % 2


def enc(z, x, y, c):
    return ((z % 4 * 4 + x % 4) * 2 + y) * 2 + c


def moved(i, second, first, dy, dc):
    z, x, y, c = dec(i)
    c = c ^ dc
    y = y ^ dy
    if c == 0:
        return enc(z + second, x + first, y, c)
    return enc(z + first, x + second, y, c)


def pairs_to(second, first, dy, dc):
    return [(i, moved(i, second, first, dy, dc)) for i in range(64)]


def send(value, second=0, first=0, dy=0, dc=0):
    return lax.ppermute(value, "term", pairs_to(second, first, dy, dc))


ORDER = np.array(
    [
        [moved(i, b, a, y, c) for c in range(2) for b in range(4) for a in range(4) for y in range(2)]
        for i in range(64)
    ],
    np.int32,
)


def gather_nodes(own):
    pair = jnp.stack([own, send(own, dy=1)])
    ring = jnp.stack([pair] + [send(pair, first=-a) for a in (1, 2, 3)]).reshape(8, 192, 128)
    plane = [ring] + [send(ring, second=-b) for b in (1, 2, 3)]
    return plane + [send(block, dc=1) for block in plane]


def reduce_nodes(blocks, root):
    root = root + send(root, dc=1)
    kept = [blocks[b] + send(blocks[4 + b], dc=1) for b in range(4)]
    got = [
        send(jnp.concatenate([kept[b].reshape(-1, 128), root]), second=b) for b in (1, 2, 3)
    ]
    kept = kept[0].reshape(4, 2, 192, 128) + sum(
        g[: 8 * 192].reshape(4, 2, 192, 128) for g in got
    )
    root = root + sum(g[8 * 192 :] for g in got)
    got = [
        send(jnp.concatenate([kept[a].reshape(-1, 128), root]), first=a) for a in (1, 2, 3)
    ]
    kept = kept[0] + sum(g[: 2 * 192].reshape(2, 192, 128) for g in got)
    root = root + sum(g[2 * 192 :] for g in got)
    got = send(jnp.concatenate([kept[1], root]), dy=1)
    return kept[0] + got[:192], root + got[192:]


def select_mode(library, op_index, active, mode_number):
    chosen = lax.dynamic_slice_in_dim(library[mode_number], op_index[mode_number] * 64, 64, 1)
    return jnp.where(active[mode_number] == 1, chosen, jnp.eye(64, dtype=chosen.dtype))


def local(
    lower_nodes, upper_nodes, root_coefficient_grid, mode_ops, op_table, leaf_active, term_coef
):
    own = jnp.concatenate([lower_nodes[0, 0], upper_nodes[0, 0]])
    pieces = gather_nodes(own)
    order = jnp.asarray(ORDER)[lax.axis_index("term")]
    onehot = (order[:, None] == jnp.arange(64)[None, :]).astype(jnp.float32)

    def reorder(matrix):
        return jnp.einsum("ri,ij,sj->rs", onehot, matrix, onehot, precision=EXACT)

    first_mode, second_mode, third_mode = [], [], []
    for t in range(2):
        index, active = op_table[t, 0], leaf_active[t, 0]
        first_mode.append(reorder(select_mode(mode_ops[0], index, active, 0)))
        second_mode.append(select_mode(mode_ops[0], index, active, 1))
        third_mode.append(reorder(select_mode(mode_ops[0], index, active, 2)))
    first_mode, second_mode, third_mode = map(
        jnp.concatenate, (first_mode, second_mode, third_mode)
    )
    level_one, level_two, moveds, images = climb(first_mode, second_mode, third_mode, pieces)
    opposite = lax.ppermute(level_one, "branch", [(0, 1), (1, 0)])
    is_first = (lax.axis_index("branch") == 0).astype(jnp.int32).reshape(1)
    root_part, *blocks = descend(
        is_first, term_coef, level_one, opposite, root_coefficient_grid, level_two, moveds, images, pieces
    )
    grads, root_image = reduce_nodes(blocks, root_part)
    return grads[None, None, :64], grads[None, None, 64:], root_image


def solution(mesh):
    in_specs = (
        P("branch", "term", None, None),
        P("branch", "term", None, None),
        P(),
        P("branch", None, None, None),
        P("term", "branch", None),
        P("term", "branch", None),
        P("term"),
    )
    out_specs = (P("branch", "term", None, None), P("branch", "term", None, None), P())
    return jax.shard_map(local, mesh=mesh, in_specs=in_specs, out_specs=out_specs, check_vma=False)
```
